512 devices in a mesh: rep: 16 (over x_lo, z), fsdp: 32 (over y, x_hi, core).
Axes of the slice: x: 4 (x_hi: 2, x_lo: 2; x = x_hi * 2 + x_lo), y: 8, z: 8, core: 2. Of those that a mesh axis runs over, the one named last changes fastest.
Arguments:
- hidden: bfloat16 [65536, 8192], P(('rep', 'fsdp')), may hold values from -24 to 24
- gain: float32 [8192], replicated, may hold values from 0.1 to 1.9
- key_weight: bfloat16 [16, 8192, 512], P('rep', 'fsdp'), may hold values from -6 to 6
- moment: float32 [16, 8192, 512], P('rep', 'fsdp'), may hold values from -4 to 4
- second: float32 [16, 8192, 512], P('rep', 'fsdp'), may hold values from 0.05 to 1
- dkeys: bfloat16 [65536, 512], P(('rep', 'fsdp')), may hold values from -6 to 6
- step: int32 [], replicated, may hold values from 0 to 29
Outputs:
- keys: bfloat16 [65536, 512], P(('rep', 'fsdp'))
- new_weight: bfloat16 [16, 8192, 512], P('rep', 'fsdp')
- new_moment: float32 [16, 8192, 512], P('rep', 'fsdp')
- new_second: float32 [16, 8192, 512], P('rep', 'fsdp')
The draws below stay inside these ranges and needn't reach their ends.
All inputs are finite; a program needn't handle non-finite values.
Results may differ from the reference program's by a relative error of at most 0.0051.
Values may be sent and summed in bfloat16 or wider, within the bound.
No kernel may reach another device: no remote copies, remote signals or barrier semaphores. Data moves between devices by JAX's collectives and lax.ppermute only.
A program may use at most 64 MiB of HBM per device.

```python
import math
import jax
import jax.numpy as jnp
from jax import lax

D = 8192
HEAD = 128
TOK_DEV = 128
KVW = 512
TOKENS = 65536
N_REP = 16
N_FSDP = 32


def strengthened(drawn, key, source, target, shards_of, factor):
    def block_of(dim):
        return (jnp.arange(drawn.shape[dim]) // (drawn.shape[dim] // shards_of)).reshape((-1,) + (1,) * (drawn.ndim - 1 - dim))

    near = jax.random.permutation(key, shards_of)[block_of(target)]
    second = (block_of(target) + shards_of // 2) % shards_of
    return jnp.where((block_of(source) == near) | (block_of(source) == second), factor * drawn, drawn)


def levels(rng, dims, pieces, low, largest):
    def one(axis_at, blocks):
        heights = jax.random.uniform(jax.random.fold_in(jax.random.fold_in(rng, 6), axis_at), (blocks,), jnp.float32, low / len(pieces), largest / len(pieces))
        return jnp.repeat(jnp.exp(heights), dims[axis_at] // blocks).reshape((-1,) + (1,) * (len(dims) - axis_at - 1))

    loudness = one(*pieces[0])
    for cut in pieces[1:]:
        loudness = loudness * one(*cut)
    return loudness


def centred(stream_key, shape, width, reach, cuts=(), kind=jnp.bfloat16):
    entries = width * jax.random.normal(stream_key, shape, jnp.float32)
    if cuts:
        entries = entries * levels(stream_key, shape, cuts, -0.22, 0.18)
    return jnp.clip(entries, -reach, reach).astype(kind)


def noise_with(stream_key, dims, spread, bound, pieces, heavy, held_as=jnp.bfloat16):
    values = spread * jax.random.normal(stream_key, dims, jnp.float32)
    if pieces:
        values = values * levels(stream_key, dims, pieces, -0.22, 0.18)
    return jnp.clip(strengthened(values, jax.random.fold_in(stream_key, 3), *heavy), -bound, bound).astype(held_as)


def setup_inputs(seed: int = 0) -> dict:
    keys = jax.random.split(jax.random.key(seed), 8)
    hidden = noise_with(keys[0], (TOKENS, D), 1.0, 24.0, ((0, 512),), (0, 1, 512, 6.0))
    gain = jnp.clip(1.0 + 0.18 * jax.random.normal(keys[1], (D,), jnp.float32), 0.1, 1.9)
    key_weight = centred(keys[2], (N_REP, D, KVW), 1.0, 6.0, ((0, 16), (1, 32)))
    moment = centred(keys[3], (N_REP, D, KVW), 0.3, 4.0, ((0, 16), (1, 32)), jnp.float32)
    second = jnp.clip(jnp.exp(math.log(1.0) - 2.9957323 * jax.random.uniform(keys[4], (N_REP, D, KVW), jnp.float32) ** levels(keys[4], (N_REP, D, KVW), ((0, 16), (1, 32)), -0.2, 0.2)), 0.05, 1.0)
    dkeys = centred(keys[5], (TOKENS, KVW), 1.0, 6.0, ((0, 512),))
    step = jax.random.randint(keys[6], (), 0, 30).astype(jnp.int32)
    return {"hidden": hidden, "gain": gain, "key_weight": key_weight, "moment": moment, "second": second, "dkeys": dkeys, "step": step}


def rotate(values, positions, sign):
    count = values.shape[0]
    heads = values.reshape(count, -1, HEAD)
    half = HEAD // 2
    freq = jnp.exp(jnp.arange(half).astype(jnp.float32) * (-2.0 * math.log(500000.0) / HEAD))
    angle = positions.astype(jnp.float32)[:, None] * freq[None, :]
    cosine = jnp.cos(angle)[:, None, :]
    sine = jnp.sin(angle)[:, None, :]
    first = heads[..., :half]
    latter = heads[..., half:]
    turned = jnp.concatenate([first * cosine - sign * latter * sine, latter * cosine + sign * first * sine], axis=-1)
    return turned.reshape(count, -1)

def reference(hidden, gain, key_weight, moment, second, dkeys, step):
    group_rows = TOK_DEV * N_FSDP
    scale = D ** (-0.5)
    positions = jnp.arange(group_rows).astype(jnp.int32)

    def one_group(items):
        rows, weight, cotangent = items
        values = rows.astype(jnp.float32)
        inverse = lax.rsqrt(lax.optimization_barrier(jnp.mean(values * values, axis=-1, keepdims=True)) + 1e-05)
        normed = (values * inverse * gain).astype(jnp.bfloat16)
        pre = jnp.dot(normed, weight, preferred_element_type=jnp.float32) * scale
        turned = rotate(pre, positions, 1.0).astype(jnp.bfloat16)
        dpre = rotate(cotangent.astype(jnp.float32), positions, -1.0).astype(jnp.bfloat16)
        grad = lax.dot_general(normed, dpre, (((0,), (0,)), ((), ())), preferred_element_type=jnp.float32) * scale
        return (turned, grad)
    turned, grads = lax.map(one_group, (hidden.reshape(N_REP, group_rows, D), key_weight, dkeys.reshape(N_REP, group_rows, KVW)))
    count = (step + 1).astype(jnp.float32)
    new_moment = 0.9 * moment + 0.1 * grads
    new_second = 0.95 * second + 0.05 * grads * grads
    mhat = new_moment / (1.0 - jnp.power(jnp.float32(0.9), count))
    vhat = new_second / (1.0 - jnp.power(jnp.float32(0.95), count))
    weight32 = key_weight.astype(jnp.float32)
    local = (weight32 - 0.05 * (mhat / (jnp.sqrt(vhat) + 1e-08) + 0.1 * weight32)).astype(jnp.bfloat16)
    phase = step % 3
    distance = jnp.where(phase == 0, 1, jnp.where(phase == 1, 2, 4)).astype(jnp.int32) % N_REP
    partner_index = (jnp.arange(N_REP).astype(jnp.int32) - distance) % N_REP
    other = jnp.take(local, partner_index, axis=0)
    new_weight = ((local.astype(jnp.float32) + other.astype(jnp.float32)) * 0.5).astype(jnp.bfloat16)
    return (turned.reshape(TOKENS, KVW), new_weight, new_moment, new_second)
```

```python
import functools
import math

import jax
import jax.numpy as jnp
from jax import lax
from jax.experimental import pallas as pl
from jax.experimental.pallas import tpu as pltpu
from jax.sharding import Mesh
from jax.sharding import PartitionSpec as P

HEAD = 128
NY, NP = 8, 4
GROUP = ("y", "x", "c")
PLANE = ("x", "c")
EVERY = ("rep", "y", "x", "c")
FAR = (4, 3, 5)
NEAR = (2, 6, 1, 7, 0)
BF16, F32 = jnp.bfloat16, jnp.float32


def up(block):
    return lax.ppermute(block, "y", [(i, (i + 1) % NY) for i in range(NY)])


def down(block):
    return lax.ppermute(block, "y", [(i, (i - 1) % NY) for i in range(NY)])


def across(block, axis):
    return lax.ppermute(block, axis, [(0, 1), (1, 0)])


def vmem(count):
    return [pl.BlockSpec(memory_space=pltpu.VMEM)] * count


def put_blocks(y, rows_ref, inverse, gain_ref, order, out_ref):
    feat = out_ref.shape[2] // len(order)
    for place, k in enumerate(order):
        block = lax.rem(y + k, NY)
        for p in range(NP):
            start = pl.multiple_of((block * NP + p) * feat, 128)
            values = rows_ref[:, pl.ds(start, feat)].astype(F32)
            normed = values * inverse * gain_ref[:, pl.ds(start, feat)]
            out_ref[p, :, place * feat : (place + 1) * feat] = normed.astype(BF16)


def norm_far_kernel(y_ref, rows_ref, gain_ref, out_ref, inverse_ref):
    values = rows_ref[...].astype(F32)
    mean = jnp.mean(values * values, axis=-1, keepdims=True)
    inverse = lax.rsqrt(mean + 1e-05)
    inverse_ref[...] = jnp.broadcast_to(inverse, inverse_ref.shape)
    put_blocks(y_ref[0], rows_ref, inverse, gain_ref, FAR, out_ref)


def norm_near_kernel(y_ref, rows_ref, gain_ref, inverse_ref, out_ref):
    put_blocks(y_ref[0], rows_ref, inverse_ref[:, :1], gain_ref, NEAR, out_ref)


def norm_far(y, hidden, gain):
    rows, width = hidden.shape
    feat = width // (NY * NP)
    step = 32
    return pl.pallas_call(
        norm_far_kernel,
        grid=(rows // step,),
        in_specs=[
            pl.BlockSpec(memory_space=pltpu.SMEM),
            pl.BlockSpec((step, width), lambda i: (i, 0)),
            pl.BlockSpec((1, width), lambda i: (0, 0)),
        ],
        out_specs=[
            pl.BlockSpec((NP, step, len(FAR) * feat), lambda i: (0, i, 0)),
            pl.BlockSpec((step, 128), lambda i: (i, 0)),
        ],
        out_shape=[
            jax.ShapeDtypeStruct((NP, rows, len(FAR) * feat), BF16),
            jax.ShapeDtypeStruct((rows, 128), F32),
        ],
        cost_estimate=pl.CostEstimate(flops=6 * rows * width, bytes_accessed=4 * rows * width, transcendentals=rows),
        name="norm_far",
    )(y, hidden, gain)


def norm_near(y, hidden, gain, inverse):
    rows, width = hidden.shape
    feat = width // (NY * NP)
    step = 32
    return pl.pallas_call(
        norm_near_kernel,
        grid=(rows // step,),
        in_specs=[
            pl.BlockSpec(memory_space=pltpu.SMEM),
            pl.BlockSpec((step, width), lambda i: (i, 0)),
            pl.BlockSpec((1, width), lambda i: (0, 0)),
            pl.BlockSpec((step, 128), lambda i: (i, 0)),
        ],
        out_specs=pl.BlockSpec((NP, step, len(NEAR) * feat), lambda i: (0, i, 0)),
        out_shape=jax.ShapeDtypeStruct((NP, rows, len(NEAR) * feat), BF16),
        cost_estimate=pl.CostEstimate(flops=3 * rows * width, bytes_accessed=4 * rows * width, transcendentals=0),
        name="norm_near",
    )(y, hidden, gain, inverse)


def turn(values, cosine, sine):
    return values * cosine + pltpu.roll(values, HEAD // 2, 1) * sine


def turn_back_kernel(values_ref, cosine_ref, sine_ref, out_ref):
    for h in range(values_ref.shape[1] // HEAD):
        cols = slice(h * HEAD, (h + 1) * HEAD)
        out_ref[:, cols] = turn(values_ref[:, cols].astype(F32), cosine_ref[...], -sine_ref[...]).astype(BF16)


def turn_back(values, cosine, sine):
    return pl.pallas_call(
        turn_back_kernel,
        in_specs=vmem(3),
        out_specs=pl.BlockSpec(memory_space=pltpu.VMEM),
        out_shape=jax.ShapeDtypeStruct(values.shape, BF16),
        cost_estimate=pl.CostEstimate(flops=4 * values.size, bytes_accessed=4 * values.size, transcendentals=0),
        name="turn_back",
    )(values, cosine, sine)


def keys_kernel(scale, parts_ref, cosine_ref, sine_ref, out_ref):
    for h in range(out_ref.shape[1] // HEAD):
        cols = slice(h * HEAD, (h + 1) * HEAD)
        total = parts_ref[0, :, cols].astype(F32)
        for p in range(1, NP):
            total = total + parts_ref[p, :, cols].astype(F32)
        out_ref[:, cols] = turn(total * scale, cosine_ref[...], sine_ref[...]).astype(BF16)


def finish_keys(parts, cosine, sine, scale):
    return pl.pallas_call(
        functools.partial(keys_kernel, scale),
        in_specs=vmem(3),
        out_specs=pl.BlockSpec(memory_space=pltpu.VMEM),
        out_shape=jax.ShapeDtypeStruct(parts.shape[1:], BF16),
        cost_estimate=pl.CostEstimate(flops=8 * parts.size, bytes_accessed=2 * parts.size, transcendentals=0),
        name="finish_keys",
    )(parts, cosine, sine)


def forward_kernel(far_ref, near_ref, w4a_ref, w4b_ref, w3, w5, w2, w6, w1, w7, w0, out_ref):
    feat = w0.shape[0]
    half = feat // 2
    rows = out_ref.shape[1]
    for p in range(NP):
        mine = slice(p * rows, (p + 1) * rows)
        total = jnp.dot(far_ref[mine, :half], w4a_ref[...], preferred_element_type=F32)
        total += jnp.dot(far_ref[mine, half:feat], w4b_ref[...], preferred_element_type=F32)
        for place, w in ((1, w3), (2, w5)):
            total += jnp.dot(far_ref[mine, place * feat : (place + 1) * feat], w[...], preferred_element_type=F32)
        for place, w in enumerate((w2, w6, w1, w7, w0)):
            total += jnp.dot(near_ref[mine, place * feat : (place + 1) * feat], w[...], preferred_element_type=F32)
        out_ref[p] = total.astype(out_ref.dtype)


def forward(far, near, weights, kind):
    tokens = far.shape[0]
    kvw = weights[-1].shape[1]
    return pl.pallas_call(
        forward_kernel,
        in_specs=vmem(2 + len(weights)),
        out_specs=pl.BlockSpec(memory_space=pltpu.VMEM),
        out_shape=jax.ShapeDtypeStruct((NP, tokens // NP, kvw), kind),
        cost_estimate=pl.CostEstimate(flops=2 * tokens * 2048 * kvw, bytes_accessed=5 << 20, transcendentals=0),
        name="forward",
    )(far, near, *weights)


def rotation(positions):
    half = HEAD // 2
    freq = jnp.exp(jnp.arange(half).astype(F32) * (-2.0 * math.log(500000.0) / HEAD))
    angle = positions.astype(F32)[:, None] * freq[None, :]
    cosine, sine = jnp.cos(angle), jnp.sin(angle)
    return jnp.concatenate([cosine, cosine], 1), jnp.concatenate([-sine, sine], 1)


def gathered_over_plane(block):
    x, c = lax.axis_index("x"), lax.axis_index("c")
    beside = across(block, "x")
    pair = jnp.stack([jnp.where(x == 0, block, beside), jnp.where(x == 0, beside, block)])
    other = across(pair, "c")
    first, second = jnp.where(c == 0, pair, other), jnp.where(c == 0, other, pair)
    return jnp.stack([first, second], 1).reshape(-1, block.shape[1])


def per_device(hidden, gain, key_weight, moment, second, dkeys, step):
    rows, width = hidden.shape
    scale = width ** (-0.5)
    weight = key_weight[0]
    feat, kvw = weight.shape
    y = lax.axis_index("y").astype(jnp.int32).reshape(1)
    positions = lax.axis_index(GROUP) * rows + jnp.arange(rows)
    cosine, sine = rotation(positions)
    dpre = gathered_over_plane(turn_back(dkeys, cosine, sine))

    gain = gain.reshape(1, -1)
    far, inverse = norm_far(y, hidden, gain)
    far = lax.all_to_all(far, PLANE, 0, 0, tiled=True).reshape(NP * rows, -1)
    near = norm_near(y, hidden, gain, inverse)
    near = lax.all_to_all(near, PLANE, 0, 0, tiled=True).reshape(NP * rows, -1)

    w1, w7 = down(weight), up(weight)
    w2, w6 = down(w1), up(w7)
    w3, w5 = down(w2), up(w6)
    w4a, w4b = down(w3[: feat // 2]), up(w5[feat // 2 :])

    def partial_grads(slices):
        total = lax.dot_general(slices, dpre, (((0,), (0,)), ((), ())), preferred_element_type=F32)
        return total.reshape(-1, feat, kvw)

    half = kvw // 2
    g4, g3, g5 = partial_grads(far)
    g2, g6, g1, g7, g0 = partial_grads(near)
    a = up(g4[:, :half].astype(BF16))
    b = down(g4[:, half:].astype(BF16))
    a = jnp.concatenate([g3[:, :half] + a.astype(F32), g3[:, half:]], 1)
    b = jnp.concatenate([g5[:, :half], g5[:, half:] + b.astype(F32)], 1)
    a, b = up(a.astype(BF16)), down(b.astype(BF16))
    a, b = up((g2 + a.astype(F32)).astype(BF16)), down((g6 + b.astype(F32)).astype(BF16))
    a, b = up((g1 + a.astype(F32)).astype(BF16)), down((g7 + b.astype(F32)).astype(BF16))
    grad = (g0 + a.astype(F32) + b.astype(F32)) * scale

    count = (step + 1).astype(F32)
    new_moment = 0.9 * moment[0] + 0.1 * grad
    new_second = 0.95 * second[0] + 0.05 * grad * grad
    mhat = new_moment / (1.0 - jnp.power(F32(0.9), count))
    vhat = new_second / (1.0 - jnp.power(F32(0.95), count))
    weight32 = weight.astype(F32)
    local = (weight32 - 0.05 * (mhat / (jnp.sqrt(vhat) + 1e-08) + 0.1 * weight32)).astype(BF16)

    parts = forward(far, near, (w4a, w4b, w3, w5, w2, w6, w1, w7, weight), BF16)
    parts = lax.all_to_all(parts, PLANE, 0, 0, tiled=True)
    keys = finish_keys(parts, cosine, sine, scale)

    groups = lax.axis_size("rep")

    def behind(distance):
        route = [((i - distance) % groups, i) for i in range(groups)]
        return lambda block: lax.ppermute(block, "rep", route)

    other = lax.switch(step % 3, [behind(1), behind(2), behind(4)], local)
    new_weight = ((local.astype(F32) + other.astype(F32)) * 0.5).astype(BF16)
    return (keys, new_weight[None], new_moment[None], new_second[None])


def solution(mesh):
    finer = Mesh(mesh.devices.reshape(mesh.shape["rep"], NY, 2, 2), EVERY)
    placed = (
        P(EVERY, None),
        P(),
        P("rep", GROUP, None),
        P("rep", GROUP, None),
        P("rep", GROUP, None),
        P(EVERY, None),
        P(),
    )
    return jax.shard_map(
        per_device,
        mesh=finer,
        in_specs=placed,
        out_specs=(P(EVERY, None), P("rep", GROUP, None), P("rep", GROUP, None), P("rep", GROUP, None)),
        check_vma=False,
    )
```

```python
import functools
import math

import jax
import jax.numpy as jnp
from jax import lax
from jax.experimental import pallas as pl
from jax.experimental.pallas import tpu as pltpu
from jax.sharding import Mesh
from jax.sharding import PartitionSpec as P


HEAD = 128
NY, NP = 8, 4
GROUP = ("y", "x", "c")
PLANE = ("x", "c")
EVERY = ("rep", "y", "x", "c")
CHUNKS = ((4, 5, 3), (6, 2, 7, 1, 0))
DISTANCES = (1, 2, 4)
BF16, F32 = jnp.bfloat16, jnp.float32


def up(block):
    return lax.ppermute(block, "y", [(i, (i + 1) % NY) for i in range(NY)])


def down(block):
    return lax.ppermute(block, "y", [(i, (i - 1) % NY) for i in range(NY)])


def vmem(count):
    return [pl.BlockSpec(memory_space=pltpu.VMEM)] * count


def put_blocks(y, rows_ref, inverse, gain_ref, order, out_ref):
    feat = rows_ref.shape[1] // (NY * NP)
    for place, k in enumerate(order):
        block = lax.rem(y + k, NY)
        for p in range(NP):
            start = pl.multiple_of((block * NP + p) * feat, 128)
            values = rows_ref[:, pl.ds(start, feat)].astype(F32)
            normed = values * inverse * gain_ref[:, pl.ds(start, feat)]
            out_ref[p, :, place * feat : (place + 1) * feat] = normed.astype(BF16)


def turn(values, cosine, sine):
    return values * cosine + pltpu.roll(values, HEAD // 2, 1) * sine


def first_kernel(y_ref, rows_ref, gain_ref, dkeys_ref, cosine_ref, sine_ref, out_ref, inverse_ref):
    values = rows_ref[...].astype(F32)
    mean = jnp.mean(values * values, axis=-1, keepdims=True)
    inverse = lax.rsqrt(mean + 1e-05)
    inverse_ref[...] = jnp.broadcast_to(inverse, inverse_ref.shape)
    put_blocks(y_ref[0], rows_ref, inverse, gain_ref, CHUNKS[0], out_ref)
    kvw = dkeys_ref.shape[1]
    offset = out_ref.shape[2] - kvw
    for h in range(kvw // HEAD):
        cols = slice(h * HEAD, (h + 1) * HEAD)
        turned = turn(dkeys_ref[:, cols].astype(F32), cosine_ref[...], -sine_ref[...]).astype(BF16)
        for p in range(NP):
            out_ref[p, :, offset + h * HEAD : offset + (h + 1) * HEAD] = turned


def later_kernel(y_ref, rows_ref, gain_ref, inverse_ref, out_ref):
    put_blocks(y_ref[0], rows_ref, inverse_ref[:, :1], gain_ref, CHUNKS[1], out_ref)


def first_chunk(y, hidden, gain, dkeys, cosine, sine):
    rows, width = hidden.shape
    kvw = dkeys.shape[1]
    span = len(CHUNKS[0]) * (width // (NY * NP)) + kvw
    step = 32
    return pl.pallas_call(
        first_kernel,
        grid=(rows // step,),
        in_specs=[
            pl.BlockSpec(memory_space=pltpu.SMEM),
            pl.BlockSpec((step, width), lambda i: (i, 0)),
            pl.BlockSpec((1, width), lambda i: (0, 0)),
            pl.BlockSpec((step, kvw), lambda i: (i, 0)),
            pl.BlockSpec((step, HEAD), lambda i: (i, 0)),
            pl.BlockSpec((step, HEAD), lambda i: (i, 0)),
        ],
        out_specs=[
            pl.BlockSpec((NP, step, span), lambda i: (0, i, 0)),
            pl.BlockSpec((step, 128), lambda i: (i, 0)),
        ],
        out_shape=[
            jax.ShapeDtypeStruct((NP, rows, span), BF16),
            jax.ShapeDtypeStruct((rows, 128), F32),
        ],
        cost_estimate=pl.CostEstimate(flops=6 * rows * width, bytes_accessed=4 * rows * width, transcendentals=rows),
        name="first_chunk",
    )(y, hidden, gain, dkeys, cosine, sine)


def later_chunk(y, hidden, gain, inverse):
    rows, width = hidden.shape
    span = len(CHUNKS[1]) * (width // (NY * NP))
    step = 32
    return pl.pallas_call(
        later_kernel,
        grid=(rows // step,),
        in_specs=[
            pl.BlockSpec(memory_space=pltpu.SMEM),
            pl.BlockSpec((step, width), lambda i: (i, 0)),
            pl.BlockSpec((1, width), lambda i: (0, 0)),
            pl.BlockSpec((step, 128), lambda i: (i, 0)),
        ],
        out_specs=pl.BlockSpec((NP, step, span), lambda i: (0, i, 0)),
        out_shape=jax.ShapeDtypeStruct((NP, rows, span), BF16),
        cost_estimate=pl.CostEstimate(flops=3 * rows * width, bytes_accessed=4 * rows * width, transcendentals=0),
        name="later_chunk",
    )(y, hidden, gain, inverse)


def keys_kernel(scale, parts_ref, cosine_ref, sine_ref, out_ref):
    for h in range(out_ref.shape[1] // HEAD):
        cols = slice(h * HEAD, (h + 1) * HEAD)
        total = parts_ref[0, :, cols].astype(F32)
        for p in range(1, NP):
            total = total + parts_ref[p, :, cols].astype(F32)
        out_ref[:, cols] = turn(total * scale, cosine_ref[...], sine_ref[...]).astype(BF16)


def finish_keys(parts, cosine, sine, scale):
    return pl.pallas_call(
        functools.partial(keys_kernel, scale),
        in_specs=vmem(3),
        out_specs=pl.BlockSpec(memory_space=pltpu.VMEM),
        out_shape=jax.ShapeDtypeStruct(parts.shape[1:], BF16),
        cost_estimate=pl.CostEstimate(flops=8 * parts.size, bytes_accessed=2 * parts.size, transcendentals=0),
        name="finish_keys",
    )(parts, cosine, sine)


def forward_kernel(core_ref, *refs):
    chunk_refs, (w0, w4, pair_ref, quad_ref), out_ref = refs[: len(CHUNKS)], refs[len(CHUNKS) : -1], refs[-1]
    feat = w0.shape[0]
    rows = out_ref.shape[1]
    place = {k: (ref, i) for ref, order in zip(chunk_refs, CHUNKS) for i, k in enumerate(order)}

    def whole(sign):
        held = [(0, w0[...]), (4, w4[...])]
        held += [((sign * 2 + k) % NY, pair_ref[i]) for i, k in enumerate((0, 4))]
        held += [((sign + k) % NY, quad_ref[i]) for i, k in enumerate((0, 4, sign * 2, sign * 2 + 4))]
        for p in range(NP):
            total = jnp.zeros((rows, w0.shape[1]), F32)
            for k, weight in held:
                ref, i = place[k]
                tokens = ref[p * rows : (p + 1) * rows, i * feat : (i + 1) * feat]
                total += jnp.dot(tokens, weight, preferred_element_type=F32)
            out_ref[p] = total.astype(out_ref.dtype)

    pl.when(core_ref[0] == 0)(lambda: whole(1))
    pl.when(core_ref[0] == 1)(lambda: whole(-1))


def forward(core, chunks, weights, kind):
    tokens = chunks[0].shape[0]
    kvw = weights[0].shape[1]
    return pl.pallas_call(
        forward_kernel,
        in_specs=[pl.BlockSpec(memory_space=pltpu.SMEM)] + vmem(len(chunks) + len(weights)),
        out_specs=pl.BlockSpec(memory_space=pltpu.VMEM),
        out_shape=jax.ShapeDtypeStruct((NP, tokens // NP, kvw), kind),
        cost_estimate=pl.CostEstimate(flops=2 * tokens * 2048 * kvw, bytes_accessed=5 << 20, transcendentals=0),
        name="forward",
    )(core, *chunks, *weights)


def rotation(positions):
    half = HEAD // 2
    freq = jnp.exp(jnp.arange(half).astype(F32) * (-2.0 * math.log(500000.0) / HEAD))
    angle = positions.astype(F32)[:, None] * freq[None, :]
    cosine, sine = jnp.cos(angle), jnp.sin(angle)
    return jnp.concatenate([cosine, cosine], 1), jnp.concatenate([-sine, sine], 1)


def toward(block, distance):
    route = []
    for y in range(NY):
        for c in range(2):
            sender = (y + distance if c == 0 else y - distance) % NY
            route.append((sender * 2 + c, y * 2 + c))
    return lax.ppermute(block, ("y", "c"), route)


def one_distance(number, hidden, gain, key_weight, moment, second, dkeys, step):
    rows, width = hidden.shape
    scale = width ** (-0.5)
    weight = key_weight[0]
    feat, kvw = weight.shape
    y = lax.axis_index("y").astype(jnp.int32).reshape(1)
    core = lax.axis_index("c").astype(jnp.int32).reshape(1)

    def exchanged(block):
        return lax.all_to_all(block, PLANE, 0, 0, tiled=True)

    positions = lax.axis_index(GROUP) * rows + jnp.arange(rows)
    cosine, sine = rotation(positions)
    gain = gain.reshape(1, -1)
    first, inverse = first_chunk(y, hidden, gain, dkeys, cosine, sine)
    first = exchanged(first).reshape(NP * rows, -1)
    later = later_chunk(y, hidden, gain, inverse)
    later = exchanged(later).reshape(NP * rows, -1)
    chunks = (first, later)
    dpre = first[:, -kvw:]

    w4 = lax.ppermute(weight, "y", [(i, (i + 4) % NY) for i in range(NY)])
    pair = toward(jnp.stack([weight, w4]), 2)
    quad = toward(jnp.concatenate([jnp.stack([weight, w4]), pair]), 1)

    def partial_grad(k):
        slices, order = (first, CHUNKS[0]) if k in CHUNKS[0] else (later, CHUNKS[1])
        place = order.index(k) * feat
        slices = slices[:, place : place + feat]
        return lax.dot_general(slices, dpre, (((0,), (0,)), ((), ())), preferred_element_type=F32)

    def added(k, arrived):
        return (partial_grad(k) + arrived.astype(F32)).astype(BF16)

    a = up(partial_grad(4).astype(BF16))
    b = down(partial_grad(5).astype(BF16))
    a = up(added(3, a))
    b = down(added(6, b))
    a = up(added(2, a))
    b = down(added(7, b))
    a = up(added(1, a))
    grad = (partial_grad(0) + a.astype(F32) + b.astype(F32)) * scale

    parts = forward(core, chunks, (weight, w4, pair, quad), BF16)
    parts = exchanged(parts)
    keys = finish_keys(parts, cosine, sine, scale)

    count = (step + 1).astype(F32)
    new_moment = 0.9 * moment[0] + 0.1 * grad
    new_second = 0.95 * second[0] + 0.05 * grad * grad
    mhat = new_moment / (1.0 - jnp.power(F32(0.9), count))
    vhat = new_second / (1.0 - jnp.power(F32(0.95), count))
    weight32 = weight.astype(F32)
    local = (weight32 - 0.05 * (mhat / (jnp.sqrt(vhat) + 1e-08) + 0.1 * weight32)).astype(BF16)
    groups = lax.axis_size("rep")
    distance = DISTANCES[number]
    other = lax.ppermute(local, "rep", [((i - distance) % groups, i) for i in range(groups)])
    new_weight = ((local.astype(F32) + other.astype(F32)) * 0.5).astype(BF16)
    return (keys, new_weight[None], new_moment[None], new_second[None])


def per_device(*args):
    def branch(number):
        def run(*args):
            return one_distance(number, *args)

        return run

    return lax.switch(args[-1] % len(DISTANCES), [branch(n) for n in range(len(DISTANCES))], *args)


def solution(mesh):
    finer = Mesh(mesh.devices.reshape(mesh.shape["rep"], NY, 2, 2), EVERY)
    placed = (
        P(EVERY, None),
        P(),
        P("rep", GROUP, None),
        P("rep", GROUP, None),
        P("rep", GROUP, None),
        P(EVERY, None),
        P(),
    )
    return jax.shard_map(
        per_device,
        mesh=finer,
        in_specs=placed,
        out_specs=(P(EVERY, None), P("rep", GROUP, None), P("rep", GROUP, None), P("rep", GROUP, None)),
        check_vma=False,
    )
```

```python
import functools
import math

import jax
import jax.numpy as jnp
from jax import lax
from jax.experimental import pallas as pl
from jax.experimental.pallas import tpu as pltpu
from jax.sharding import Mesh
from jax.sharding import PartitionSpec as P


HEAD = 128
NY, NP = 8, 4
GROUP = ("y", "x", "c")
PLANE = ("x", "c")
EVERY = ("rep", "y", "x", "c")
DISTANCES = (1, 2, 4)
SENDS = (1, 2, 3, 4, 7, 6, 5)
BF16, F32 = jnp.bfloat16, jnp.float32


def shifted(block, distance):
    return lax.ppermute(block, "y", [(i, (i + distance) % NY) for i in range(NY)])


def across(block, axis):
    return lax.ppermute(block, axis, [(0, 1), (1, 0)])


def vmem(count):
    return [pl.BlockSpec(memory_space=pltpu.VMEM)] * count


SMEM = pl.BlockSpec(memory_space=pltpu.SMEM)


def cost(flops, nbytes):
    return pl.CostEstimate(flops=flops, bytes_accessed=nbytes, transcendentals=0)


def turn(values, cosine, sine):
    return values * cosine + pltpu.roll(values, HEAD // 2, 1) * sine


def norm_kernel(y_ref, rows_ref, gain_ref, out_ref):
    values = rows_ref[...].astype(F32)
    inverse = lax.rsqrt(jnp.mean(values * values, axis=-1, keepdims=True) + 1e-05)
    feat = rows_ref.shape[1] // (NY * NP)
    for k in range(NY):
        block = lax.rem(y_ref[0] + k, NY)
        for p in range(NP):
            start = pl.multiple_of((block * NP + p) * feat, 128)
            part = rows_ref[:, pl.ds(start, feat)].astype(F32)
            normed = part * inverse * gain_ref[:, pl.ds(start, feat)]
            out_ref[p, :, k * feat : (k + 1) * feat] = normed.astype(BF16)


def norm(y, hidden, gain):
    rows, width = hidden.shape
    step = 32
    return pl.pallas_call(
        norm_kernel,
        grid=(rows // step,),
        in_specs=[SMEM, pl.BlockSpec((step, width), lambda i: (i, 0)), pl.BlockSpec((1, width), lambda i: (0, 0))],
        out_specs=pl.BlockSpec((NP, step, width // NP), lambda i: (0, i, 0)),
        out_shape=jax.ShapeDtypeStruct((NP, rows, width // NP), BF16),
        cost_estimate=cost(6 * rows * width, 4 * rows * width),
        name="norm",
    )(y, hidden, gain)


def turn_back_kernel(values_ref, cosine_ref, sine_ref, out_ref):
    for h in range(values_ref.shape[1] // HEAD):
        cols = slice(h * HEAD, (h + 1) * HEAD)
        turned = turn(values_ref[:, cols].astype(F32), cosine_ref[...], -sine_ref[...])
        out_ref[cols, :] = turned.T.astype(BF16)


def turn_back(values, cosine, sine):
    return pl.pallas_call(
        turn_back_kernel,
        in_specs=vmem(3),
        out_specs=pl.BlockSpec(memory_space=pltpu.VMEM),
        out_shape=jax.ShapeDtypeStruct(values.shape[::-1], BF16),
        cost_estimate=cost(4 * values.size, 4 * values.size),
        name="turn_back",
    )(values, cosine, sine)


def grads_kernel(at_ref, tokens_ref, d00, d10, d01, d11, *refs):
    outs, dpre_ref = refs[:-1], refs[-1]
    rows = d00.shape[1]
    for i, piece in enumerate((d00, d10, d01, d11)):
        dpre_ref[:, pl.ds(pl.multiple_of(at_ref[i] * rows, 128), rows)] = piece[...]
    feat = outs[0].shape[1]
    for k, out in enumerate(outs):
        block = tokens_ref[:, k * feat : (k + 1) * feat]
        out[...] = jnp.dot(dpre_ref[...], block, preferred_element_type=F32).astype(out.dtype)


def grads(at, tokens, pieces):
    count, width = tokens.shape
    kvw = pieces[0].shape[0]
    feat = width // NY
    return pl.pallas_call(
        grads_kernel,
        in_specs=[SMEM] + vmem(1 + len(pieces)),
        out_specs=vmem(NY),
        out_shape=[jax.ShapeDtypeStruct((kvw, feat), BF16 if k else F32) for k in range(NY)],
        scratch_shapes=[pltpu.VMEM((kvw, count), BF16)],
        cost_estimate=cost(2 * count * width * kvw, 2 * count * width + 3 * width * kvw),
        name="grads",
    )(at, tokens, *pieces)


def forward_kernel(tokens_ref, *refs):
    weights, out_ref = refs[:-1], refs[-1]
    feat = weights[0].shape[0]
    rows = out_ref.shape[1]
    for p in range(NP):
        mine = slice(p * rows, (p + 1) * rows)
        total = jnp.zeros(out_ref.shape[1:], F32)
        for k, weight in enumerate(weights):
            total += jnp.dot(tokens_ref[mine, k * feat : (k + 1) * feat], weight[...], preferred_element_type=F32)
        out_ref[p] = total.astype(out_ref.dtype)


def forward(tokens, weights):
    count, width = tokens.shape
    kvw = weights[0].shape[1]
    return pl.pallas_call(
        forward_kernel,
        in_specs=vmem(1 + len(weights)),
        out_specs=pl.BlockSpec(memory_space=pltpu.VMEM),
        out_shape=jax.ShapeDtypeStruct((NP, count // NP, kvw), BF16),
        cost_estimate=cost(2 * count * width * kvw, 5 << 20),
        name="forward",
    )(tokens, *weights)


def keys_kernel(scale, parts_ref, cosine_ref, sine_ref, out_ref):
    for h in range(out_ref.shape[1] // HEAD):
        cols = slice(h * HEAD, (h + 1) * HEAD)
        total = parts_ref[0, :, cols].astype(F32)
        for p in range(1, NP):
            total = total + parts_ref[p, :, cols].astype(F32)
        out_ref[:, cols] = turn(total * scale, cosine_ref[...], sine_ref[...]).astype(BF16)


def finish_keys(parts, cosine, sine, scale):
    return pl.pallas_call(
        functools.partial(keys_kernel, scale),
        in_specs=vmem(3),
        out_specs=pl.BlockSpec(memory_space=pltpu.VMEM),
        out_shape=jax.ShapeDtypeStruct(parts.shape[1:], BF16),
        cost_estimate=cost(8 * parts.size, 2 * parts.size),
        name="finish_keys",
    )(parts, cosine, sine)


def update_kernel(scale, bias_ref, moment_ref, second_ref, weight_ref, *refs):
    arrived, (moment_out, second_out, local_out) = refs[:-3], refs[-3:]
    total = arrived[0][...]
    for part in arrived[1:]:
        total = total + part[...].astype(F32)
    grad = total.T * scale
    moment = 0.9 * moment_ref[...] + 0.1 * grad
    second = 0.95 * second_ref[...] + 0.05 * grad * grad
    moment_out[...] = moment
    second_out[...] = second
    mhat = moment / bias_ref[0]
    vhat = second / bias_ref[1]
    weight = weight_ref[...].astype(F32)
    local_out[...] = (weight - 0.05 * (mhat / (jnp.sqrt(vhat) + 1e-08) + 0.1 * weight)).astype(BF16)


def update(bias, moment, second, weight, arrived, scale):
    feat, kvw = weight.shape
    step = 128
    flat = pl.BlockSpec((step, kvw), lambda i: (i, 0))
    turned = pl.BlockSpec((kvw, step), lambda i: (0, i))
    return pl.pallas_call(
        functools.partial(update_kernel, scale),
        grid=(feat // step,),
        in_specs=[SMEM] + [flat] * 3 + [turned] * len(arrived),
        out_specs=[flat] * 3,
        out_shape=[jax.ShapeDtypeStruct((feat, kvw), kind) for kind in (F32, F32, BF16)],
        cost_estimate=cost(30 * feat * kvw, 34 * feat * kvw),
        name="update",
    )(bias, moment, second, weight, *arrived)


def rotation(positions):
    half = HEAD // 2
    freq = jnp.exp(jnp.arange(half).astype(F32) * (-2.0 * math.log(500000.0) / HEAD))
    angle = positions.astype(F32)[:, None] * freq[None, :]
    cosine, sine = jnp.cos(angle), jnp.sin(angle)
    return jnp.concatenate([cosine, cosine], 1), jnp.concatenate([-sine, sine], 1)


def one_distance(number, hidden, gain, key_weight, moment, second, dkeys, step):
    rows, width = hidden.shape
    scale = width ** (-0.5)
    weight = key_weight[0]
    y, x, c = [lax.axis_index(axis).astype(jnp.int32) for axis in GROUP]

    tokens = norm(y.reshape(1), hidden, gain.reshape(1, -1))
    tokens = lax.all_to_all(tokens, PLANE, 0, 0, tiled=True).reshape(NP * rows, -1)

    positions = lax.axis_index(GROUP) * rows + jnp.arange(rows)
    cosine, sine = rotation(positions)
    own = turn_back(dkeys, cosine, sine)
    beside = across(own, "x")
    other = across(own, "c")
    corner = across(beside, "c")

    held = {0: weight}
    for k in (1, 2, 3, 4):
        held[NY - k] = shifted(held[(NY + 1 - k) % NY], 1)
        if k < 4:
            held[k] = shifted(held[k - 1], -1)

    at = jnp.stack([x * 2 + c, (1 - x) * 2 + c, x * 2 + 1 - c, (1 - x) * 2 + 1 - c])
    blocks = grads(at, tokens, (own, beside, other, corner))
    arrived = [blocks[0]]
    for k in SENDS:
        arrived.append(shifted(blocks[k], k))

    parts = forward(tokens, [held[k] for k in range(NY)])
    parts = lax.all_to_all(parts, PLANE, 0, 0, tiled=True)
    keys = finish_keys(parts, cosine, sine, scale)

    count = (step + 1).astype(F32)
    bias = jnp.stack([1.0 - jnp.power(F32(0.9), count), 1.0 - jnp.power(F32(0.95), count)])
    new_moment, new_second, local = update(bias, moment[0], second[0], weight, arrived, scale)
    groups = lax.axis_size("rep")
    distance = DISTANCES[number]
    other = lax.ppermute(local, "rep", [((i - distance) % groups, i) for i in range(groups)])
    new_weight = ((local.astype(F32) + other.astype(F32)) * 0.5).astype(BF16)
    return (keys, new_weight[None], new_moment[None], new_second[None])


def per_device(*args):
    def branch(number):
        def run(*args):
            return one_distance(number, *args)

        return run

    return lax.switch(args[-1] % len(DISTANCES), [branch(n) for n in range(len(DISTANCES))], *args)


def solution(mesh):
    finer = Mesh(mesh.devices.reshape(mesh.shape["rep"], NY, 2, 2), EVERY)
    placed = (
        P(EVERY, None),
        P(),
        P("rep", GROUP, None),
        P("rep", GROUP, None),
        P("rep", GROUP, None),
        P(EVERY, None),
        P(),
    )
    return jax.shard_map(
        per_device,
        mesh=finer,
        in_specs=placed,
        out_specs=(P(EVERY, None), P("rep", GROUP, None), P("rep", GROUP, None), P("rep", GROUP, None)),
        check_vma=False,
    )
```

```python
import functools
import math

import jax
import jax.numpy as jnp
from jax import lax
from jax.experimental import pallas as pl
from jax.experimental.pallas import tpu as pltpu
from jax.sharding import Mesh
from jax.sharding import PartitionSpec as P


HEAD = 128
NY, NP = 4, 8
GROUP = ("y", "h", "x", "c")
PLANE = ("h", "x", "c")
EVERY = ("rep", "y", "h", "x", "c")
DISTANCES = (1, 2, 4)
SENDS = (1, 3, 2)
BF16, F32 = jnp.bfloat16, jnp.float32


def shifted(block, distance):
    return lax.ppermute(block, "y", [(i, (i + distance) % NY) for i in range(NY)])


def toward(block):
    route = []
    for y in range(NY):
        for c in range(2):
            sender = (y + 1 if c == 0 else y - 1) % NY
            route.append((sender * 2 + c, y * 2 + c))
    return lax.ppermute(block, ("y", "c"), route)


def across(block, axis):
    return lax.ppermute(block, axis, [(0, 1), (1, 0)])


def vmem(count):
    return [pl.BlockSpec(memory_space=pltpu.VMEM)] * count


SMEM = pl.BlockSpec(memory_space=pltpu.SMEM)


def cost(flops, nbytes):
    return pl.CostEstimate(flops=flops, bytes_accessed=nbytes, transcendentals=0)


def turn(values, cosine, sine):
    return values * cosine + pltpu.roll(values, HEAD // 2, 1) * sine


def norm_kernel(y_ref, rows_ref, gain_ref, out_ref):
    values = rows_ref[...].astype(F32)
    inverse = lax.rsqrt(jnp.mean(values * values, axis=-1, keepdims=True) + 1e-05)
    feat = rows_ref.shape[1] // (NY * NP)
    for k in range(NY):
        block = lax.rem(y_ref[0] + k, NY)
        for p in range(NP):
            start = pl.multiple_of((block * NP + p) * feat, 128)
            part = rows_ref[:, pl.ds(start, feat)].astype(F32)
            normed = part * inverse * gain_ref[:, pl.ds(start, feat)]
            out_ref[p, :, k * feat : (k + 1) * feat] = normed.astype(BF16)


def norm(y, hidden, gain):
    rows, width = hidden.shape
    step = 32
    return pl.pallas_call(
        norm_kernel,
        grid=(rows // step,),
        in_specs=[SMEM, pl.BlockSpec((step, width), lambda i: (i, 0)), pl.BlockSpec((1, width), lambda i: (0, 0))],
        out_specs=pl.BlockSpec((NP, step, width // NP), lambda i: (0, i, 0)),
        out_shape=jax.ShapeDtypeStruct((NP, rows, width // NP), BF16),
        cost_estimate=cost(6 * rows * width, 4 * rows * width),
        name="norm",
    )(y, hidden, gain)


def turn_back_kernel(at_ref, own_ref, beside_ref, two_ref, four_ref, cosine_ref, sine_ref, out_ref):
    pieces = [own_ref, beside_ref, *(two_ref.at[i] for i in range(2)), *(four_ref.at[i] for i in range(4))]
    rows, kvw = own_ref.shape
    for i, piece in enumerate(pieces):
        start = pl.multiple_of(at_ref[i] * rows, 128)
        cosine, sine = cosine_ref[pl.ds(start, rows), :], sine_ref[pl.ds(start, rows), :]
        for h in range(kvw // HEAD):
            cols = slice(h * HEAD, (h + 1) * HEAD)
            turned = turn(piece[:, cols].astype(F32), cosine, -sine)
            out_ref[cols, pl.ds(start, rows)] = turned.T.astype(BF16)


def turn_back(at, pieces, cosine, sine):
    rows, kvw = pieces[0].shape
    return pl.pallas_call(
        turn_back_kernel,
        in_specs=[SMEM] + vmem(len(pieces) + 2),
        out_specs=pl.BlockSpec(memory_space=pltpu.VMEM),
        out_shape=jax.ShapeDtypeStruct((kvw, NP * rows), BF16),
        cost_estimate=cost(8 * NP * rows * kvw, 6 * NP * rows * kvw),
        name="turn_back",
    )(at, *pieces, cosine, sine)


def grads_kernel(tokens_ref, dpre_ref, *outs):
    feat = outs[0].shape[1]
    for k, out in enumerate(outs):
        block = tokens_ref[:, k * feat : (k + 1) * feat]
        out[...] = jnp.dot(dpre_ref[...], block, preferred_element_type=F32).astype(out.dtype)


def grads(tokens, dpre):
    count, width = tokens.shape
    kvw = dpre.shape[0]
    feat = width // NY
    return pl.pallas_call(
        grads_kernel,
        in_specs=vmem(2),
        out_specs=vmem(NY),
        out_shape=[jax.ShapeDtypeStruct((kvw, feat), BF16 if k else F32) for k in range(NY)],
        cost_estimate=cost(2 * count * width * kvw, 2 * count * width + 3 * width * kvw),
        name="grads",
    )(tokens, dpre)


def forward_kernel(core_ref, tokens_ref, w0, w2, pair_ref, out_ref):
    feat = w0.shape[0]
    rows = out_ref.shape[1]
    here = pl.multiple_of((1 + 2 * core_ref[0]) * feat, 128)
    there = pl.multiple_of((3 - 2 * core_ref[0]) * feat, 128)
    for p in range(NP):
        mine = slice(p * rows, (p + 1) * rows)

        def term(start, weight):
            return jnp.dot(tokens_ref[mine, pl.ds(start, feat)], weight, preferred_element_type=F32)

        total = term(0, w0[...]) + term(2 * feat, w2[...]) + term(here, pair_ref[0]) + term(there, pair_ref[1])
        out_ref[p] = total.astype(out_ref.dtype)


def forward(core, tokens, weights):
    count, width = tokens.shape
    kvw = weights[0].shape[1]
    return pl.pallas_call(
        forward_kernel,
        in_specs=[SMEM] + vmem(1 + len(weights)),
        out_specs=pl.BlockSpec(memory_space=pltpu.VMEM),
        out_shape=jax.ShapeDtypeStruct((NP, count // NP, kvw), BF16),
        cost_estimate=cost(2 * count * width * kvw, 5 << 20),
        name="forward",
    )(core, tokens, *weights)


def keys_kernel(scale, parts_ref, cosine_ref, sine_ref, out_ref):
    for h in range(out_ref.shape[1] // HEAD):
        cols = slice(h * HEAD, (h + 1) * HEAD)
        total = parts_ref[0, :, cols].astype(F32)
        for p in range(1, NP):
            total = total + parts_ref[p, :, cols].astype(F32)
        out_ref[:, cols] = turn(total * scale, cosine_ref[...], sine_ref[...]).astype(BF16)


def finish_keys(parts, cosine, sine, scale):
    return pl.pallas_call(
        functools.partial(keys_kernel, scale),
        in_specs=vmem(3),
        out_specs=pl.BlockSpec(memory_space=pltpu.VMEM),
        out_shape=jax.ShapeDtypeStruct(parts.shape[1:], BF16),
        cost_estimate=cost(8 * parts.size, 2 * parts.size),
        name="finish_keys",
    )(parts, cosine, sine)


def update_kernel(scale, bias_ref, moment_ref, second_ref, weight_ref, *refs):
    arrived, (moment_out, second_out, local_out) = refs[:-3], refs[-3:]
    total = arrived[0][...]
    for part in arrived[1:]:
        total = total + part[...].astype(F32)
    grad = total.T * scale
    moment = 0.9 * moment_ref[...] + 0.1 * grad
    second = 0.95 * second_ref[...] + 0.05 * grad * grad
    moment_out[...] = moment
    second_out[...] = second
    mhat = moment / bias_ref[0]
    vhat = second / bias_ref[1]
    weight = weight_ref[...].astype(F32)
    local_out[...] = (weight - 0.05 * (mhat / (jnp.sqrt(vhat) + 1e-08) + 0.1 * weight)).astype(BF16)


def update(bias, moment, second, weight, arrived, scale):
    feat, kvw = weight.shape
    step = 128
    flat = pl.BlockSpec((step, kvw), lambda i: (i, 0))
    turned = pl.BlockSpec((kvw, step), lambda i: (0, i))
    return pl.pallas_call(
        functools.partial(update_kernel, scale),
        grid=(feat // step,),
        in_specs=[SMEM] + [flat] * 3 + [turned] * len(arrived),
        out_specs=[flat] * 3,
        out_shape=[jax.ShapeDtypeStruct((feat, kvw), kind) for kind in (F32, F32, BF16)],
        cost_estimate=cost(30 * feat * kvw, 34 * feat * kvw),
        name="update",
    )(bias, moment, second, weight, *arrived)


def rotation(positions):
    half = HEAD // 2
    freq = jnp.exp(jnp.arange(half).astype(F32) * (-2.0 * math.log(500000.0) / HEAD))
    angle = positions.astype(F32)[:, None] * freq[None, :]
    cosine, sine = jnp.cos(angle), jnp.sin(angle)
    return jnp.concatenate([cosine, cosine], 1), jnp.concatenate([-sine, sine], 1)


def one_distance(number, hidden, gain, key_weight, moment, second, dkeys, step):
    rows, width = hidden.shape
    scale = width ** (-0.5)
    weight = key_weight[0]
    y, h, x, c = [lax.axis_index(axis).astype(jnp.int32) for axis in GROUP]

    beside = across(dkeys, "h")
    tokens = norm(y.reshape(1), hidden, gain.reshape(1, -1))
    two = across(jnp.stack([dkeys, beside]), "x")
    tokens = lax.all_to_all(tokens, PLANE, 0, 0, tiled=True).reshape(NP * rows, -1)
    four = across(jnp.concatenate([jnp.stack([dkeys, beside]), two]), "c")
    cosine, sine = rotation(y * NP * rows + jnp.arange(NP * rows))
    at = jnp.stack(
        [(h ^ dh) * 4 + (x ^ dx) * 2 + (c ^ dc) for dc in (0, 1) for dx in (0, 1) for dh in (0, 1)]
    )
    dpre = turn_back(at, (dkeys, beside, two, four), cosine, sine)
    start = at[0] * rows
    cosine, sine = [lax.dynamic_slice_in_dim(table, start, rows) for table in (cosine, sine)]

    w2 = shifted(weight, 2)
    pair = toward(jnp.stack([weight, w2]))

    blocks = grads(tokens, dpre)
    arrived = [blocks[0]]
    for k in SENDS:
        arrived.append(shifted(blocks[k], k))

    parts = forward(c.reshape(1), tokens, (weight, w2, pair))
    parts = lax.all_to_all(parts, PLANE, 0, 0, tiled=True)
    keys = finish_keys(parts, cosine, sine, scale)

    count = (step + 1).astype(F32)
    bias = jnp.stack([1.0 - jnp.power(F32(0.9), count), 1.0 - jnp.power(F32(0.95), count)])
    new_moment, new_second, local = update(bias, moment[0], second[0], weight, arrived, scale)
    groups = lax.axis_size("rep")
    distance = DISTANCES[number]
    other = lax.ppermute(local, "rep", [((i - distance) % groups, i) for i in range(groups)])
    new_weight = ((local.astype(F32) + other.astype(F32)) * 0.5).astype(BF16)
    return (keys, new_weight[None], new_moment[None], new_second[None])


def per_device(*args):
    def branch(number):
        def run(*args):
            return one_distance(number, *args)

        return run

    return lax.switch(args[-1] % len(DISTANCES), [branch(n) for n in range(len(DISTANCES))], *args)


def solution(mesh):
    finer = Mesh(mesh.devices.reshape(mesh.shape["rep"], NY, 2, 2, 2), EVERY)
    placed = (
        P(EVERY, None),
        P(),
        P("rep", GROUP, None),
        P("rep", GROUP, None),
        P("rep", GROUP, None),
        P(EVERY, None),
        P(),
    )
    return jax.shard_map(
        per_device,
        mesh=finer,
        in_specs=placed,
        out_specs=(P(EVERY, None), P("rep", GROUP, None), P("rep", GROUP, None), P("rep", GROUP, None)),
        check_vma=False,
    )
```

```python
import functools
import math

import jax
import jax.numpy as jnp
from jax import lax
from jax.experimental import pallas as pl
from jax.experimental.pallas import tpu as pltpu
from jax.sharding import Mesh
from jax.sharding import PartitionSpec as P


HEAD = 128
NY, NP = 4, 8
GROUP = ("y", "h", "x", "c")
PLANE = ("h", "x", "c")
EVERY = ("rep", "y", "h", "x", "c")
DISTANCES = (1, 2, 4)
CHUNKS = ((2, 1), (3, 0))
SENDS = (2, 1, 3)
BF16, F32 = jnp.bfloat16, jnp.float32


def shifted(block, distance):
    return lax.ppermute(block, "y", [(i, (i + distance) % NY) for i in range(NY)])


def toward(block):
    route = []
    for y in range(NY):
        for c in range(2):
            sender = (y + 1 if c == 0 else y - 1) % NY
            route.append((sender * 2 + c, y * 2 + c))
    return lax.ppermute(block, ("y", "c"), route)


def across(block, axis):
    return lax.ppermute(block, axis, [(0, 1), (1, 0)])


def vmem(count):
    return [pl.BlockSpec(memory_space=pltpu.VMEM)] * count


SMEM = pl.BlockSpec(memory_space=pltpu.SMEM)


def cost(flops, nbytes):
    return pl.CostEstimate(flops=flops, bytes_accessed=nbytes, transcendentals=0)


def turn(values, cosine, sine):
    return values * cosine + pltpu.roll(values, HEAD // 2, 1) * sine


def put_blocks(y, order, rows_ref, inverse, gain_ref, out_ref):
    feat = rows_ref.shape[1] // (NY * NP)
    for place, k in enumerate(order):
        block = lax.rem(y + k, NY)
        for p in range(NP):
            start = pl.multiple_of((block * NP + p) * feat, 128)
            part = rows_ref[:, pl.ds(start, feat)].astype(F32)
            normed = part * inverse * gain_ref[:, pl.ds(start, feat)]
            out_ref[p, :, place * feat : (place + 1) * feat] = normed.astype(BF16)


def norm_first_kernel(y_ref, rows_ref, gain_ref, out_ref, inverse_ref):
    values = rows_ref[...].astype(F32)
    inverse = lax.rsqrt(jnp.mean(values * values, axis=-1, keepdims=True) + 1e-05)
    inverse_ref[...] = jnp.broadcast_to(inverse, inverse_ref.shape)
    put_blocks(y_ref[0], CHUNKS[0], rows_ref, inverse, gain_ref, out_ref)


def norm_second_kernel(y_ref, rows_ref, gain_ref, inverse_ref, out_ref):
    put_blocks(y_ref[0], CHUNKS[1], rows_ref, inverse_ref[:, :1], gain_ref, out_ref)


def norm(y, hidden, gain, inverse=None):
    rows, width = hidden.shape
    step = 32
    span = 2 * (width // (NY * NP))
    in_specs = [SMEM, pl.BlockSpec((step, width), lambda i: (i, 0)), pl.BlockSpec((1, width), lambda i: (0, 0))]
    out_spec = pl.BlockSpec((NP, step, span), lambda i: (0, i, 0))
    out_shape = jax.ShapeDtypeStruct((NP, rows, span), BF16)
    stat_spec = pl.BlockSpec((step, 128), lambda i: (i, 0))
    shared = dict(grid=(rows // step,), cost_estimate=cost(4 * rows * width, 3 * rows * width))
    if inverse is None:
        return pl.pallas_call(
            norm_first_kernel,
            in_specs=in_specs,
            out_specs=[out_spec, stat_spec],
            out_shape=[out_shape, jax.ShapeDtypeStruct((rows, 128), F32)],
            name="norm_first",
            **shared,
        )(y, hidden, gain)
    return pl.pallas_call(
        norm_second_kernel,
        in_specs=in_specs + [stat_spec],
        out_specs=out_spec,
        out_shape=out_shape,
        name="norm_second",
        **shared,
    )(y, hidden, gain, inverse)


def turn_back_kernel(at_ref, own_ref, beside_ref, two_ref, four_ref, cosine_ref, sine_ref, out_ref):
    pieces = [own_ref, beside_ref, *(two_ref.at[i] for i in range(2)), *(four_ref.at[i] for i in range(4))]
    rows, kvw = own_ref.shape
    for i, piece in enumerate(pieces):
        start = pl.multiple_of(at_ref[i] * rows, 128)
        cosine, sine = cosine_ref[pl.ds(start, rows), :], sine_ref[pl.ds(start, rows), :]
        for h in range(kvw // HEAD):
            cols = slice(h * HEAD, (h + 1) * HEAD)
            turned = turn(piece[:, cols].astype(F32), cosine, -sine)
            out_ref[cols, pl.ds(start, rows)] = turned.T.astype(BF16)


def turn_back(at, pieces, cosine, sine):
    rows, kvw = pieces[0].shape
    return pl.pallas_call(
        turn_back_kernel,
        in_specs=[SMEM] + vmem(len(pieces) + 2),
        out_specs=pl.BlockSpec(memory_space=pltpu.VMEM),
        out_shape=jax.ShapeDtypeStruct((kvw, NP * rows), BF16),
        cost_estimate=cost(8 * NP * rows * kvw, 6 * NP * rows * kvw),
        name="turn_back",
    )(at, *pieces, cosine, sine)


def grads_kernel(tokens_ref, dpre_ref, *outs):
    feat = outs[0].shape[1]
    for place, out in enumerate(outs):
        block = tokens_ref[:, place * feat : (place + 1) * feat]
        out[...] = jnp.dot(dpre_ref[...], block, preferred_element_type=F32).astype(out.dtype)


def grads(tokens, dpre, order):
    count, width = tokens.shape
    kvw = dpre.shape[0]
    feat = width // len(order)
    return pl.pallas_call(
        grads_kernel,
        in_specs=vmem(2),
        out_specs=vmem(len(order)),
        out_shape=[jax.ShapeDtypeStruct((kvw, feat), BF16 if k else F32) for k in order],
        cost_estimate=cost(2 * count * width * kvw, 2 * count * width + 3 * width * kvw),
        name="grads",
    )(tokens, dpre)


def forward_kernel(core_ref, a_ref, b_ref, w0, w2, pair_ref, out_ref):
    feat = w0.shape[0]
    rows = out_ref.shape[1]
    core = core_ref[0]
    w1 = pair_ref[core]
    w3 = pair_ref[1 - core]
    held = {0: w0[...], 1: w1, 2: w2[...], 3: w3}
    for p in range(NP):
        mine = slice(p * rows, (p + 1) * rows)
        total = jnp.zeros(out_ref.shape[1:], F32)
        for ref, order in zip((a_ref, b_ref), CHUNKS):
            for place, k in enumerate(order):
                total += jnp.dot(ref[mine, place * feat : (place + 1) * feat], held[k], preferred_element_type=F32)
        out_ref[p] = total.astype(out_ref.dtype)


def forward(core, chunks, weights):
    count, kvw = chunks[0].shape[0], weights[0].shape[1]
    flops = 2 * count * kvw * sum(chunk.shape[1] for chunk in chunks)
    return pl.pallas_call(
        forward_kernel,
        in_specs=[SMEM] + vmem(len(chunks) + len(weights)),
        out_specs=pl.BlockSpec(memory_space=pltpu.VMEM),
        out_shape=jax.ShapeDtypeStruct((NP, count // NP, kvw), BF16),
        cost_estimate=cost(flops, 5 << 20),
        name="forward",
    )(core, *chunks, *weights)


def keys_kernel(scale, parts_ref, cosine_ref, sine_ref, out_ref):
    for h in range(out_ref.shape[1] // HEAD):
        cols = slice(h * HEAD, (h + 1) * HEAD)
        total = parts_ref[0, :, cols].astype(F32)
        for p in range(1, NP):
            total = total + parts_ref[p, :, cols].astype(F32)
        out_ref[:, cols] = turn(total * scale, cosine_ref[...], sine_ref[...]).astype(BF16)


def finish_keys(parts, cosine, sine, scale):
    return pl.pallas_call(
        functools.partial(keys_kernel, scale),
        in_specs=vmem(3),
        out_specs=pl.BlockSpec(memory_space=pltpu.VMEM),
        out_shape=jax.ShapeDtypeStruct(parts.shape[1:], BF16),
        cost_estimate=cost(8 * parts.size, 2 * parts.size),
        name="finish_keys",
    )(parts, cosine, sine)


def update_kernel(scale, bias_ref, moment_ref, second_ref, weight_ref, *refs):
    arrived, (moment_out, second_out, local_out) = refs[:-3], refs[-3:]
    total = arrived[0][...]
    for part in arrived[1:]:
        total = total + part[...].astype(F32)
    grad = total.T * scale
    moment = 0.9 * moment_ref[...] + 0.1 * grad
    second = 0.95 * second_ref[...] + 0.05 * grad * grad
    moment_out[...] = moment
    second_out[...] = second
    mhat = moment / bias_ref[0]
    vhat = second / bias_ref[1]
    weight = weight_ref[...].astype(F32)
    local_out[...] = (weight - 0.05 * (mhat / (jnp.sqrt(vhat) + 1e-08) + 0.1 * weight)).astype(BF16)


def update(bias, moment, second, weight, arrived, scale):
    feat, kvw = weight.shape
    step = 128
    flat = pl.BlockSpec((step, kvw), lambda i: (i, 0))
    turned = pl.BlockSpec((kvw, step), lambda i: (0, i))
    return pl.pallas_call(
        functools.partial(update_kernel, scale),
        grid=(feat // step,),
        in_specs=[SMEM] + [flat] * 3 + [turned] * len(arrived),
        out_specs=[flat] * 3,
        out_shape=[jax.ShapeDtypeStruct((feat, kvw), kind) for kind in (F32, F32, BF16)],
        cost_estimate=cost(30 * feat * kvw, 34 * feat * kvw),
        name="update",
    )(bias, moment, second, weight, *arrived)


def rotation(positions):
    half = HEAD // 2
    freq = jnp.exp(jnp.arange(half).astype(F32) * (-2.0 * math.log(500000.0) / HEAD))
    angle = positions.astype(F32)[:, None] * freq[None, :]
    cosine, sine = jnp.cos(angle), jnp.sin(angle)
    return jnp.concatenate([cosine, cosine], 1), jnp.concatenate([-sine, sine], 1)


def one_distance(number, hidden, gain, key_weight, moment, second, dkeys, step):
    rows, width = hidden.shape
    scale = width ** (-0.5)
    weight = key_weight[0]
    y, h, x, c = [lax.axis_index(axis).astype(jnp.int32) for axis in GROUP]

    beside = across(dkeys, "h")
    at_y, gain = y.reshape(1), gain.reshape(1, -1)
    first, inverse = norm(at_y, hidden, gain)
    two = across(jnp.stack([dkeys, beside]), "x")
    first = lax.all_to_all(first, PLANE, 0, 0, tiled=True).reshape(NP * rows, -1)
    later = norm(at_y, hidden, gain, inverse)
    later = lax.all_to_all(later, PLANE, 0, 0, tiled=True).reshape(NP * rows, -1)
    four = across(jnp.concatenate([jnp.stack([dkeys, beside]), two]), "c")
    cosine, sine = rotation(y * NP * rows + jnp.arange(NP * rows))
    at = jnp.stack(
        [(h ^ dh) * 4 + (x ^ dx) * 2 + (c ^ dc) for dc in (0, 1) for dx in (0, 1) for dh in (0, 1)]
    )
    dpre = turn_back(at, (dkeys, beside, two, four), cosine, sine)
    start = at[0] * rows
    cosine, sine = [lax.dynamic_slice_in_dim(table, start, rows) for table in (cosine, sine)]

    w2 = shifted(weight, 2)
    pair = toward(jnp.stack([weight, w2]))

    blocks = {}
    for chunk, order in zip((first, later), CHUNKS):
        blocks.update(zip(order, grads(chunk, dpre, order)))
    arrived = [blocks[0]]
    for k in SENDS:
        arrived.append(shifted(blocks[k], k))

    parts = forward(c.reshape(1), (first, later), (weight, w2, pair))
    parts = lax.all_to_all(parts, PLANE, 0, 0, tiled=True)
    keys = finish_keys(parts, cosine, sine, scale)

    count = (step + 1).astype(F32)
    bias = jnp.stack([1.0 - jnp.power(F32(0.9), count), 1.0 - jnp.power(F32(0.95), count)])
    new_moment, new_second, local = update(bias, moment[0], second[0], weight, arrived, scale)
    groups = lax.axis_size("rep")
    distance = DISTANCES[number]
    other = lax.ppermute(local, "rep", [((i - distance) % groups, i) for i in range(groups)])
    new_weight = ((local.astype(F32) + other.astype(F32)) * 0.5).astype(BF16)
    return (keys, new_weight[None], new_moment[None], new_second[None])


def per_device(*args):
    def branch(number):
        def run(*args):
            return one_distance(number, *args)

        return run

    return lax.switch(args[-1] % len(DISTANCES), [branch(n) for n in range(len(DISTANCES))], *args)


def solution(mesh):
    finer = Mesh(mesh.devices.reshape(mesh.shape["rep"], NY, 2, 2, 2), EVERY)
    placed = (
        P(EVERY, None),
        P(),
        P("rep", GROUP, None),
        P("rep", GROUP, None),
        P("rep", GROUP, None),
        P(EVERY, None),
        P(),
    )
    return jax.shard_map(
        per_device,
        mesh=finer,
        in_specs=placed,
        out_specs=(P(EVERY, None), P("rep", GROUP, None), P("rep", GROUP, None), P("rep", GROUP, None)),
        check_vma=False,
    )
```
